32 devices in a mesh: seq: 8 (over z, y), tp: 4 (over x, core).
Axes of the slice: x: 2, y: 2, z: 4, core: 2. Of those that a mesh axis runs over, the one named last changes fastest.
Arguments:
- x_in: bfloat16 [1024, 8192], P('seq', 'tp'), may hold values from -6 to 6
- gate_in: bfloat16 [1024, 8192], P('seq', 'tp'), may hold values from -6 to 6
- conv_weight: float32 [4, 8192], P(None, 'tp'), may hold values from -3 to 3
- conv_bias: float32 [8192], P('tp'), may hold values from -0.5 to 0.5
- x_weight: bfloat16 [8192, 544], P('tp'), may hold values from -0.0625 to 0.0625
- dt_weight: bfloat16 [512, 8192], P(None, 'tp'), may hold values from -0.25 to 0.25
- dt_bias: float32 [8192], P('tp'), may hold values from -5 to -2.5
- decay_rate: float32 [8192, 16], P('tp'), may hold values from 0 to 4
- skip_gain: float32 [8192], P('tp'), may hold values from 0.5 to 1.5
- out_weight: bfloat16 [8192, 4096], P('tp'), may hold values from -0.0625 to 0.0625
- residual_in: bfloat16 [1024, 4096], P(('seq', 'tp')), may hold values from -36 to 36
- norm_gain: float32 [4096], replicated, may hold values from 0.1 to 1.9
- expert_ids: int32 [1024, 2], P(('seq', 'tp')), may hold values from 0 to 7, all different within a row; in each aligned block of 32 rows (0 to 31, 32 to 63, ...) at most 12 rows name the same one
- gate_prob: float32 [1024, 2], P(('seq', 'tp')), may hold values from 0.1 to 1
- up_weight: bfloat16 [4096, 98304], P(None, ('seq', 'tp')), may hold values from -0.09375 to 0.09375
- down_weight: bfloat16 [98304, 4096], P(('seq', 'tp')), may hold values from -0.0546875 to 0.0546875
Outputs:
- mixer_out: bfloat16 [1024, 4096], P(('seq', 'tp'))
- layer_out: bfloat16 [1024, 4096], P(('seq', 'tp'))
The draws below stay inside these ranges and needn't reach their ends.
Inputs may be any that keep to these rules, and one draw needn't show every extreme that they name: `expert_ids`: each row names two different experts. In each device's aligned block of 32 rows no expert is named by more than 12 rows, a bound that some block reaches.
All inputs are finite; a program needn't handle non-finite values.
Results may differ from the reference program's by a relative error of at most 0.007.
Values may be sent and summed in bfloat16 or wider, within the bound.
A program may use at most 192 MiB of HBM per device.

```python
import math
import jax
import jax.numpy as jnp
import numpy as np
from jax import lax

D = 4096
INNER = 8192
STATE = 16
DTRANK = 512
KCONV = 4
EXPERTS = 8
FF = 12288
LENGTH = 1024
ROWS = 32
CAP = 12
OWNERS = 4
FFDEV = 3072
N_SEQ = 8
N_TP = 4


def draw_decay_rate(key, part):
    base = jax.random.fold_in(key, 11)
    key_pick, key_fast, key_slow = jax.random.split(base, 3)
    share = 0.5
    quick = jax.random.uniform(key_pick, (INNER, 1), jnp.float32) < share
    fast = jnp.exp(jax.random.uniform(key_fast, (INNER, STATE), jnp.float32, math.log(0.5), math.log(4.0)))
    slow = jnp.exp(jax.random.uniform(key_slow, (INNER, STATE), jnp.float32, math.log(2.0), math.log(20.0))) / LENGTH
    return jnp.where(quick, fast, slow).astype(jnp.float32)


def draw_residual_in(key, part):
    base = jax.random.fold_in(key, 23)
    key_row, key_col, key_main = jax.random.split(base, 3)
    row_scale = jnp.exp(jax.random.uniform(key_row, (LENGTH, 1), jnp.float32, math.log(0.3), math.log(3.0)))
    col_scale = jnp.exp(jax.random.uniform(key_col, (1, D), jnp.float32, math.log(0.3), math.log(3.0)))
    values = jax.random.normal(key_main, (LENGTH, D), jnp.float32)
    values = jnp.clip(values, -4.0, 4.0)
    return (values * row_scale * col_scale).astype(jnp.bfloat16)


def levels(rng, extent, pieces, smallest, largest):
    loudness = 1.0
    for axis_at, shards_of in pieces:
        draws = jax.random.uniform(jax.random.fold_in(jax.random.fold_in(rng, 6), axis_at), (shards_of,), jnp.float32, smallest / len(pieces), largest / len(pieces))
        loudness = loudness * jnp.repeat(jnp.exp(draws), extent[axis_at] // shards_of).reshape((-1,) + (1,) * (len(extent) - 1 - axis_at))
    return loudness


def shared_out(rng, own, number, rows, count, top, bound, slope):
    sequence = jax.random.permutation(rng, count)
    crowded, common = shares(count, rows * top, bound, slope, True), shares(count, rows * top, bound, slope, False)
    places = jnp.arange(count)

    def named(lengths, offset_by):
        used = int((lengths > 0).sum())
        fixed = max(1, used // 4)
        moved = fixed + (places - fixed + offset_by * (used - fixed)) % max(1, count - fixed)
        return jnp.zeros((count,), jnp.int32).at[sequence[jnp.where(places < fixed, places, moved)]].set(jnp.asarray(lengths, jnp.int32))

    lengths = jnp.where(number % 4 == 0, named(crowded, number // 4), named(common, number - number // 4 - 1))
    mixed = jax.random.permutation(jax.random.fold_in(own, 3), count)
    source_of, receiver = mixed[0:count // 2 * 2:2], mixed[1:count // 2 * 2:2]
    slack = jnp.minimum(lengths[source_of] - 1, bound - lengths[receiver]) // 2
    slack = jnp.where((source_of == sequence[0]) | (receiver == sequence[0]) | (lengths[receiver] == 0), 0, jnp.maximum(slack, 0))
    moved = jax.random.randint(jax.random.fold_in(own, 4), (count // 2,), 0, 1 << 20) % (slack + 1)
    lengths = lengths.at[source_of].add(-moved).at[receiver].add(moved)
    labels = jnp.searchsorted(jnp.cumsum(lengths), jnp.arange(rows * top), side="right").astype(jnp.int32)
    listing = labels.reshape(top, rows).T
    listing = listing[jax.random.permutation(jax.random.fold_in(own, 1), rows)]
    offset_by = jax.random.randint(jax.random.fold_in(own, 2), (rows, 1), 0, top)
    return jnp.take_along_axis(listing, (jnp.arange(top)[None, :] + offset_by) % top, axis=1)


def shares(count, total, bound, lean, full):
    loads = [(1 << 20) // math.isqrt(standing ** lean) + 1 for standing in range(1, count + 1)]
    largest = bound if full else min(bound, max(-(-total // count), total * loads[0] // sum(loads)))
    least = 1 if total - largest >= count - 1 else 0
    given, spare = [largest] + [least] * (count - 1), total - largest - least * (count - 1)
    while spare > 0:
        movable = [i for i in range(1, count) if given[i] < largest] or [i for i in range(1, count) if given[i] < bound]
        whole, budget = sum([loads[i] for i in movable]), spare
        for i in movable:
            addition = min(bound - given[i], max(1, budget * loads[i] // whole), spare)
            given[i] = given[i] + addition
            spare = spare - addition
    return np.array(given)


def normal_values(stream_key, shape, scale, most, pieces=(), held_as=jnp.bfloat16):
    array = jax.random.normal(stream_key, shape, jnp.float32) * scale
    if len(pieces) > 0:
        array = levels(stream_key, shape, pieces, -0.22, 0.18) * array
    return jnp.clip(array, min=-most, max=most).astype(held_as)


def setup_inputs(seed: int = 0) -> dict:
    keys = jax.random.split(jax.random.key(seed), 17)
    x_in = normal_values(keys[0], (LENGTH, INNER), 1.0, 6.0, ((0, 8), (1, 4)))
    gate_in = normal_values(keys[1], (LENGTH, INNER), 1.0, 6.0, ((0, 8), (1, 4)))
    conv_weight = normal_values(keys[2], (KCONV, INNER), 0.5, 3.0, ((1, 4),), jnp.float32)
    conv_bias = jnp.clip(jax.random.uniform(keys[3], (INNER,), jnp.float32, -0.5, 0.5) * levels(keys[3], (INNER,), ((0, 4),), -0.4, 0.0), -0.5, 0.5)
    x_weight = normal_values(keys[4], (INNER, DTRANK + 2 * STATE), INNER ** -0.5, 0.0625, ((0, 4),))
    dt_weight = normal_values(keys[5], (DTRANK, INNER), DTRANK ** -0.5, 0.25, ((1, 4),))
    dt_bias = jnp.clip(-5.0 + 2.5 * jax.random.uniform(keys[6], (INNER,), jnp.float32) ** levels(keys[6], (INNER,), ((0, 4),), -0.2, 0.2), -5.0, -2.5)
    decay_rate = draw_decay_rate(jax.random.fold_in(keys[16], 71), 0)
    skip_gain = jnp.clip(0.5 + 1.0 * jax.random.uniform(keys[8], (INNER,), jnp.float32) ** levels(keys[8], (INNER,), ((0, 4),), -0.2, 0.2), 0.5, 1.5)
    out_weight = normal_values(keys[9], (INNER, D), INNER ** -0.5, 0.0625, ((0, 4),))
    residual_in = draw_residual_in(jax.random.fold_in(keys[16], 71), 0)
    norm_gain = jnp.clip(1.0 + 0.18 * jax.random.normal(keys[11], (D,), jnp.float32), 0.1, 1.9)
    expert_ids_keys = jax.random.split(jax.random.fold_in(keys[12], 1), LENGTH // ROWS)
    expert_ids_turns = jax.random.permutation(jax.random.fold_in(keys[12], 3), LENGTH // ROWS)
    expert_ids = jax.vmap(lambda own, number: shared_out(jax.random.fold_in(keys[12], 2), own, number, ROWS, EXPERTS, 2, CAP, 2))(expert_ids_keys, expert_ids_turns).reshape((LENGTH, 2))
    gate_prob = jnp.clip(0.1 + 0.9 * jax.random.uniform(keys[13], (LENGTH, 2), jnp.float32) ** levels(keys[13], (LENGTH, 2), ((0, 32),), -0.2, 0.2), 0.1, 1.0)
    up_weight = normal_values(keys[14], (D, EXPERTS * FF), D ** -0.5, 0.09375, ((1, 32),))
    down_weight = normal_values(keys[15], (EXPERTS * FF, D), FF ** -0.5, 0.0546875, ((0, 32),))
    return dict(x_in=x_in, gate_in=gate_in, conv_weight=conv_weight, conv_bias=conv_bias, x_weight=x_weight, dt_weight=dt_weight, dt_bias=dt_bias, decay_rate=decay_rate, skip_gain=skip_gain, out_weight=out_weight, residual_in=residual_in, norm_gain=norm_gain, expert_ids=expert_ids, gate_prob=gate_prob, up_weight=up_weight, down_weight=down_weight)


def reference(x_in, gate_in, conv_weight, conv_bias, x_weight, dt_weight, dt_bias, decay_rate, skip_gain, out_weight, residual_in, norm_gain, expert_ids, gate_prob, up_weight, down_weight):
    reach = KCONV - 1
    padded = jnp.concatenate([jnp.zeros((reach, INNER), jnp.float32), x_in.astype(jnp.float32)], axis=0)
    conv_out = conv_bias[None, :] + sum((conv_weight[offset][None, :] * padded[offset:offset + LENGTH] for offset in range(KCONV)))
    inner = jax.nn.silu(conv_out).astype(jnp.bfloat16)
    projected = jnp.dot(inner, x_weight, preferred_element_type=jnp.float32)
    dt_low = projected[:, :DTRANK].astype(jnp.bfloat16)
    entry_rows = projected[:, DTRANK:DTRANK + STATE]
    readout_rows = projected[:, DTRANK + STATE:]
    step_size = jax.nn.softplus(jnp.dot(dt_low, dt_weight, preferred_element_type=jnp.float32) + dt_bias[None, :])
    drive = step_size * inner.astype(jnp.float32)
    negative_rate = -decay_rate.T

    def advance(carried, columns):
        step_row, drive_row, entry_row, readout_row = columns
        carried = jnp.exp(step_row[None, :] * negative_rate) * carried + entry_row[:, None] * drive_row[None, :]
        return (carried, lax.optimization_barrier(jnp.sum(readout_row[:, None] * carried, axis=0)))
    start_state = jnp.zeros((STATE, INNER), jnp.float32)
    ssm = lax.scan(advance, start_state, (step_size, drive, entry_rows, readout_rows))[1]
    mixed = ((ssm + skip_gain[None, :] * inner.astype(jnp.float32)) * jax.nn.silu(gate_in.astype(jnp.float32))).astype(jnp.bfloat16)
    mixer_out = (jnp.dot(mixed, out_weight, preferred_element_type=jnp.float32) + residual_in.astype(jnp.float32)).astype(jnp.bfloat16)
    mixer_wide = mixer_out.astype(jnp.float32)
    normed = (mixer_wide * lax.rsqrt(lax.optimization_barrier(jnp.mean(mixer_wide * mixer_wide, axis=1, keepdims=True)) + 1e-06) * norm_gain[None, :]).astype(jnp.bfloat16)
    devices = N_SEQ * N_TP
    chosen = expert_ids.reshape(devices, ROWS * 2).astype(jnp.int32)
    expert_hits = (chosen[:, :, None] == jnp.arange(EXPERTS, dtype=jnp.int32)[None, None, :]).astype(jnp.int32)
    earlier_hits = jnp.cumsum(expert_hits, axis=1) - expert_hits
    slot_index = lax.optimization_barrier(jnp.sum(earlier_hits * expert_hits, axis=2)).astype(jnp.int32)
    device_index = jnp.arange(devices, dtype=jnp.int32)[:, None]
    row_source = (device_index * ROWS + jnp.arange(ROWS * 2, dtype=jnp.int32)[None, :] // 2).astype(jnp.int32)
    target = ((chosen * devices + device_index) * CAP + slot_index).astype(jnp.int32)
    table = jnp.full((EXPERTS * devices * CAP,), LENGTH, jnp.int32).at[target.reshape(-1)].set(row_source.reshape(-1))
    padded_rows = jnp.concatenate([normed, jnp.zeros((1, D), jnp.bfloat16)], axis=0)

    def expert(which):
        picked = lax.dynamic_slice_in_dim(table, which * devices * CAP, devices * CAP)
        rows_in = padded_rows[picked]
        up_block = lax.dynamic_slice_in_dim(up_weight, which * FF, FF, 1)
        down_block = lax.dynamic_slice_in_dim(down_weight, which * FF, FF, 0)
        hidden = jax.nn.silu(jnp.dot(rows_in, up_block, preferred_element_type=jnp.float32)).astype(jnp.bfloat16)

        def add_piece(piece, total):
            hidden_part = lax.dynamic_slice_in_dim(hidden, piece * FFDEV, FFDEV, 1)
            down_part = lax.dynamic_slice_in_dim(down_block, piece * FFDEV, FFDEV, 0)
            rounded = jnp.dot(hidden_part, down_part, preferred_element_type=jnp.float32).astype(jnp.bfloat16)
            rounded = lax.optimization_barrier(rounded)
            return total + rounded.astype(jnp.float32)
        return lax.fori_loop(0, OWNERS, add_piece, jnp.zeros((devices * CAP, D), jnp.float32))
    expert_out = lax.map(expert, jnp.arange(EXPERTS, dtype=jnp.int32))
    gathered = expert_out.reshape(EXPERTS * devices * CAP, D)[target.reshape(-1)]
    weighted = gathered.reshape(LENGTH, 2, D) * gate_prob[:, :, None]
    layer_out = (mixer_wide + lax.optimization_barrier(jnp.sum(weighted, axis=1))).astype(jnp.bfloat16)
    return (mixer_out, layer_out)
```

```python
import functools

import jax
import jax.numpy as jnp
from jax import lax
from jax.experimental import pallas as pl
from jax.experimental.pallas import tpu as pltpu
from jax.sharding import PartitionSpec as P

STATE = 16
DTRANK = 512
EXPERTS = 8
MESH = pl.DeviceIdType.MESH
VMEM_SPEC = pl.BlockSpec(memory_space=pltpu.VMEM)
SMEM_SPEC = pl.BlockSpec(memory_space=pltpu.SMEM)
F32 = jnp.float32
BF16 = jnp.bfloat16
MIB = 1024 * 1024


def shifted(value, axis, steps):
    count = lax.axis_size(axis)
    initial, last = (max(0, -steps), min(count, count - steps))
    return lax.ppermute(value, axis, [(source, source + steps) for source in range(initial, last)])


def greet(peers):
    barrier = pltpu.get_barrier_semaphore()
    for peer in peers:
        pl.semaphore_signal(barrier, inc=1, device_id=peer, device_id_type=MESH)
    pl.semaphore_wait(barrier, len(peers))


def send(source, target, send_sem, recv_sem, device):
    return pltpu.make_async_remote_copy(
        src_ref=source,
        dst_ref=target,
        send_sem=send_sem,
        recv_sem=recv_sem,
        device_id=device,
        device_id_type=MESH,
    )


def bit_of(index, stage):
    return lax.rem(index // 2**stage, 2)


def flipped(index, stage):
    return index + 2**stage - 2 * 2**stage * bit_of(index, stage)


def stages_of(count):
    return count.bit_length() - 1


def sum_kernel(count, part_ref, out_ref, outgoing, arriving, send_sems, recv_sems):
    me = lax.axis_index("tp")
    stages = stages_of(count)
    greet([{"tp": flipped(me, k)} for k in range(stages)])
    for k in range(stages):
        source = part_ref if k == 0 else outgoing
        copy = send(
            source, arriving.at[k], send_sems.at[k], recv_sems.at[k], {"tp": flipped(me, k)}
        )
        copy.start()
        copy.wait()
        total = source[...].astype(F32) + arriving[k].astype(F32)
        if k < stages - 1:
            outgoing[...] = total.astype(BF16)
        else:
            out_ref[...] = total


def sum_over_tp(part):
    count = lax.axis_size("tp")
    stages = stages_of(count)
    return pl.pallas_call(
        functools.partial(sum_kernel, count),
        out_shape=jax.ShapeDtypeStruct(part.shape, F32),
        in_specs=[VMEM_SPEC],
        out_specs=VMEM_SPEC,
        scratch_shapes=[
            pltpu.VMEM(part.shape, BF16),
            pltpu.VMEM((stages, *part.shape), BF16),
            pltpu.SemaphoreType.DMA((stages,)),
            pltpu.SemaphoreType.DMA((stages,)),
        ],
        compiler_params=pltpu.CompilerParams(collective_id=0, has_side_effects=True),
        name="projection_sum",
    )(part)


def scan_kernel(
    count,
    step_ref,
    inner_ref,
    maps_ref,
    rate_ref,
    out_ref,
    state,
    outgoing,
    arriving,
    send_sems,
    recv_sems,
):
    me = lax.axis_index("seq")
    tokens = step_ref.shape[0]
    tile = step_ref.shape[1:]
    greet([{"seq": lax.rem(me + d, count)} for d in range(1, count)])

    def advance(t, states):
        step = step_ref[t]
        drive = step * inner_ref[t]
        return step, tuple(
            jnp.exp(step * rate_ref[n]) * states[n] + maps_ref[t, n] * drive for n in range(STATE)
        )

    def ending(t, carried):
        states, total = carried
        step, states = advance(t, states)
        return states, total + step

    zero = jnp.zeros(tile, F32)
    states, total = lax.fori_loop(0, tokens, ending, ((zero,) * STATE, zero))
    for n in range(STATE):
        outgoing[n] = states[n].astype(BF16)
    upper = total.astype(BF16)
    outgoing[STATE] = upper
    outgoing[STATE + 1] = (total - upper.astype(F32)).astype(BF16)

    def copy_by(d):
        return send(
            outgoing,
            arriving.at[d],
            send_sems.at[d],
            recv_sems.at[d],
            {"seq": lax.rem(me + d, count)},
        )

    for d in range(1, count):

        @pl.when(me + d < count)
        def _():
            copy_by(d).start()

    state[...] = jnp.zeros(state.shape, F32)
    for d in range(count - 1, 0, -1):

        @pl.when(me >= d)
        def _():
            copy_by(d).wait_recv()
            passed = arriving[d, STATE].astype(F32) + arriving[d, STATE + 1].astype(F32)
            for n in range(STATE):
                state[n] = jnp.exp(passed * rate_ref[n]) * state[n] + arriving[d, n].astype(F32)

    def reading(t, states):
        _, states = advance(t, states)
        terms = [maps_ref[t, STATE + n] * states[n] for n in range(STATE)]
        while len(terms) > 1:
            terms = [a + b for a, b in zip(terms[::2], terms[1::2])]
        out_ref[t] = terms[0]
        return states

    lax.fori_loop(0, tokens, reading, tuple(state[n] for n in range(STATE)))
    for d in range(1, count):

        @pl.when(me + d < count)
        def _():
            copy_by(d).wait_send()


def recur(step_size, inner, maps, decay_rate):
    count = lax.axis_size("seq")
    tokens, channels = step_size.shape
    tile = (channels // 128, 128)
    rate = -decay_rate.T.reshape(STATE, *tile)
    out = pl.pallas_call(
        functools.partial(scan_kernel, count),
        out_shape=jax.ShapeDtypeStruct((tokens, *tile), F32),
        in_specs=[VMEM_SPEC, VMEM_SPEC, SMEM_SPEC, VMEM_SPEC],
        out_specs=VMEM_SPEC,
        scratch_shapes=[
            pltpu.VMEM((STATE, *tile), F32),
            pltpu.VMEM((STATE + 2, *tile), BF16),
            pltpu.VMEM((count, STATE + 2, *tile), BF16),
            pltpu.SemaphoreType.DMA((count,)),
            pltpu.SemaphoreType.DMA((count,)),
        ],
        compiler_params=pltpu.CompilerParams(
            collective_id=1, has_side_effects=True, vmem_limit_bytes=24 * MIB
        ),
        name="recurrence",
    )(step_size.reshape(tokens, *tile), inner.reshape(tokens, *tile), maps, rate)
    return out.reshape(tokens, channels)


def mixer_kernel(count, part_ref, residual_ref, gain_ref, mixer_ref, normed_ref, *scratch):
    stages = stages_of(count)
    works, arrivings = scratch[:stages], scratch[stages : 2 * stages]
    send_sems, recv_sems, gather_send_sems, gather_recv_sems = scratch[2 * stages :]
    me = lax.axis_index("tp")
    greet([{"tp": flipped(me, k)} for k in range(stages)])
    total = None
    for k in range(stages):
        source = part_ref if k == 0 else works[k]
        kept = count // 2 ** (k + 1)
        bit = bit_of(me, k)
        copies = [
            send(
                source.at[2 * i + 1 - bit],
                arrivings[k].at[i],
                send_sems.at[k, i],
                recv_sems.at[k, i],
                {"tp": flipped(me, k)},
            )
            for i in range(kept)
        ]
        for copy in copies:
            copy.start()
        for i, copy in enumerate(copies):
            copy.wait()
            total = source[2 * i + bit].astype(F32) + arrivings[k][i].astype(F32)
            if k < stages - 1:
                works[k + 1][i] = total.astype(BF16)
    mixer = (total + residual_ref[...].astype(F32)).astype(BF16)
    mixer_ref[...] = mixer
    wide = mixer.astype(F32)
    normed_ref[me] = (
        wide
        * lax.rsqrt(jnp.mean(wide * wide, axis=1, keepdims=True) + 1e-06)
        * gain_ref[...]
    ).astype(BF16)
    for k in range(stages - 1, -1, -1):
        low = lax.rem(me, 2 ** (k + 1))
        copies = []
        for i in range(count // 2 ** (k + 1)):
            block = normed_ref.at[low + 2 ** (k + 1) * i]
            copies.append(
                send(
                    block,
                    block,
                    gather_send_sems.at[k, i],
                    gather_recv_sems.at[k, i],
                    {"tp": flipped(me, k)},
                )
            )
        for copy in copies:
            copy.start()
        for copy in copies:
            copy.wait()


def mixer_rows(part, residual, gain):
    count = lax.axis_size("tp")
    stages = stages_of(count)
    rows, width = residual.shape
    sems = pltpu.SemaphoreType.DMA((stages, count // 2))
    return pl.pallas_call(
        functools.partial(mixer_kernel, count),
        out_shape=(
            jax.ShapeDtypeStruct((rows, width), BF16),
            jax.ShapeDtypeStruct((count, rows, width), BF16),
        ),
        in_specs=[VMEM_SPEC] * 3,
        out_specs=(VMEM_SPEC, VMEM_SPEC),
        scratch_shapes=[pltpu.VMEM((count // 2**k, rows, width), BF16) for k in range(stages)]
        + [pltpu.VMEM((count // 2 ** (k + 1), rows, width), BF16) for k in range(stages)]
        + [sems] * 4,
        compiler_params=pltpu.CompilerParams(
            collective_id=2, has_side_effects=True, vmem_limit_bytes=32 * MIB
        ),
        name="mixer_sum",
    )(part.reshape(count, rows, width), residual, gain.reshape(1, width))


def expert_share(arrived_flat, up_weight, down_weight):
    hidden = jax.nn.silu(jnp.dot(arrived_flat, up_weight, preferred_element_type=F32)).astype(BF16)
    return jnp.dot(hidden, down_weight, preferred_element_type=F32).astype(BF16)


def per_device(
    x_in,
    gate_in,
    conv_weight,
    conv_bias,
    x_weight,
    dt_weight,
    dt_bias,
    decay_rate,
    skip_gain,
    out_weight,
    residual_in,
    norm_gain,
    expert_ids,
    gate_prob,
    up_weight,
    down_weight,
):
    tokens, channels = x_in.shape
    width = out_weight.shape[1]
    reach = conv_weight.shape[0] - 1
    rim_rows = shifted(x_in[tokens - reach :], "seq", 1)
    padded = jnp.concatenate([rim_rows, x_in], axis=0).astype(F32)
    conv_out = conv_bias[None, :] + sum(
        (
            conv_weight[offset][None, :] * padded[offset : offset + tokens]
            for offset in range(reach + 1)
        )
    )
    inner = jax.nn.silu(conv_out).astype(BF16)
    projected = sum_over_tp(jnp.dot(inner, x_weight, preferred_element_type=F32).astype(BF16))
    dt_low = projected[:, :DTRANK].astype(BF16)
    step_size = jax.nn.softplus(
        jnp.dot(dt_low, dt_weight, preferred_element_type=F32) + dt_bias[None, :]
    )
    ssm = recur(step_size, inner.astype(F32), projected[:, DTRANK:], decay_rate)
    mixed = (
        (ssm + skip_gain[None, :] * inner.astype(F32)) * jax.nn.silu(gate_in.astype(F32))
    ).astype(BF16)
    rows = tokens // lax.axis_size("tp")
    mixer_out, normed_all = mixer_rows(
        jnp.dot(mixed, out_weight, preferred_element_type=F32).astype(BF16), residual_in, norm_gain
    )
    normed = lax.dynamic_index_in_dim(normed_all, lax.axis_index("tp"), 0, False)
    mixer_wide = mixer_out.astype(F32)
    seq_count = lax.axis_size("seq")
    devices = seq_count * lax.axis_size("tp")
    seq_group = seq_count // EXPERTS
    capacity = 3 * rows // EXPERTS
    chosen = expert_ids.reshape(-1)
    expert_hits = (chosen[:, None] == jnp.arange(EXPERTS, dtype=jnp.int32)[None, :]).astype(
        jnp.int32
    )
    earlier_hits = jnp.cumsum(expert_hits, axis=0) - expert_hits
    slot_index = jnp.sum(earlier_hits * expert_hits, axis=1)
    target = chosen * capacity + slot_index
    placing = (jnp.arange(EXPERTS * capacity, dtype=jnp.int32)[:, None] == target[None, :]).astype(
        jnp.bfloat16
    )
    placing = jnp.sum(placing.reshape(EXPERTS * capacity, rows, 2), axis=2)
    slots_out = (
        jnp.dot(placing, normed, preferred_element_type=jnp.float32)
        .astype(jnp.bfloat16)
        .reshape(EXPERTS, capacity, width)
    )
    along_seq = jnp.repeat(slots_out, seq_group, axis=0)
    arrived_seq = lax.all_to_all(along_seq, "seq", split_axis=0, concat_axis=0, tiled=True)
    arrived_all = lax.all_gather(
        arrived_seq.reshape(1, seq_count * capacity, width), "tp", axis=0, tiled=True
    )
    arrived_flat = arrived_all.reshape(devices * capacity, width)
    summed = lax.psum_scatter(
        expert_share(arrived_flat, up_weight, down_weight).astype(jnp.float32).astype(jnp.bfloat16),
        "tp",
        scatter_dimension=0,
        tiled=True,
    ).astype(jnp.float32)
    home = lax.all_to_all(
        summed.reshape(seq_count, capacity, width).astype(jnp.bfloat16),
        "seq",
        split_axis=0,
        concat_axis=0,
        tiled=True,
    ).astype(jnp.float32)
    expert_out = jnp.sum(home.reshape(EXPERTS, seq_group, capacity, width), axis=1).reshape(
        EXPERTS * capacity, width
    )
    picked = jnp.take(expert_out, target, axis=0).reshape(rows, 2, width)
    layer_out = (mixer_wide + jnp.sum(picked * gate_prob[:, :, None], axis=1)).astype(jnp.bfloat16)
    return (mixer_out, layer_out)


def solution(mesh):
    return jax.shard_map(
        per_device,
        mesh=mesh,
        in_specs=(
            P("seq", "tp"),
            P("seq", "tp"),
            P(None, "tp"),
            P("tp"),
            P("tp", None),
            P(None, "tp"),
            P("tp"),
            P("tp", None),
            P("tp"),
            P("tp", None),
            P(("seq", "tp"), None),
            P(),
            P(("seq", "tp"), None),
            P(("seq", "tp"), None),
            P(None, ("seq", "tp")),
            P(("seq", "tp"), None),
        ),
        out_specs=(P(("seq", "tp"), None), P(("seq", "tp"), None)),
        check_vma=False,
    )
```

```python
import functools

import jax
import jax.numpy as jnp
from jax import lax
from jax.experimental import pallas as pl
from jax.experimental.pallas import tpu as pltpu
from jax.sharding import PartitionSpec as P

STATE = 16
DTRANK = 512
EXPERTS = 8
MESH = pl.DeviceIdType.MESH
VMEM_SPEC = pl.BlockSpec(memory_space=pltpu.VMEM)
SMEM_SPEC = pl.BlockSpec(memory_space=pltpu.SMEM)
F32 = jnp.float32
BF16 = jnp.bfloat16
MIB = 1024 * 1024


def shifted(value, axis, steps):
    count = lax.axis_size(axis)
    initial, last = (max(0, -steps), min(count, count - steps))
    return lax.ppermute(value, axis, [(source, source + steps) for source in range(initial, last)])


def greet(peers):
    barrier = pltpu.get_barrier_semaphore()
    for peer in peers:
        pl.semaphore_signal(barrier, inc=1, device_id=peer, device_id_type=MESH)
    pl.semaphore_wait(barrier, len(peers))


def send(source, target, send_sem, recv_sem, device):
    return pltpu.make_async_remote_copy(
        src_ref=source,
        dst_ref=target,
        send_sem=send_sem,
        recv_sem=recv_sem,
        device_id=device,
        device_id_type=MESH,
    )


def bit_of(index, stage):
    return lax.rem(index // 2**stage, 2)


def flipped(index, stage):
    return index + 2**stage - 2 * 2**stage * bit_of(index, stage)


def stages_of(count):
    return count.bit_length() - 1


def sum_kernel(count, part_ref, out_ref, outgoing, arriving, send_sems, recv_sems):
    me = lax.axis_index("tp")
    stages = stages_of(count)
    greet([{"tp": flipped(me, k)} for k in range(stages)])
    for k in range(stages):
        source = part_ref if k == 0 else outgoing
        copy = send(
            source, arriving.at[k], send_sems.at[k], recv_sems.at[k], {"tp": flipped(me, k)}
        )
        copy.start()
        copy.wait()
        total = source[...].astype(F32) + arriving[k].astype(F32)
        if k < stages - 1:
            outgoing[...] = total.astype(BF16)
        else:
            out_ref[...] = total


def sum_over_tp(part):
    count = lax.axis_size("tp")
    stages = stages_of(count)
    return pl.pallas_call(
        functools.partial(sum_kernel, count),
        out_shape=jax.ShapeDtypeStruct(part.shape, F32),
        in_specs=[VMEM_SPEC],
        out_specs=VMEM_SPEC,
        scratch_shapes=[
            pltpu.VMEM(part.shape, BF16),
            pltpu.VMEM((stages, *part.shape), BF16),
            pltpu.SemaphoreType.DMA((stages,)),
            pltpu.SemaphoreType.DMA((stages,)),
        ],
        compiler_params=pltpu.CompilerParams(collective_id=0, has_side_effects=True),
        name="projection_sum",
    )(part)


def scan_kernel(
    count,
    step_ref,
    inner_ref,
    maps_ref,
    rate_ref,
    out_ref,
    state,
    outgoing,
    arriving,
    send_sems,
    recv_sems,
):
    me = lax.axis_index("seq")
    tokens = step_ref.shape[0]
    tile = step_ref.shape[1:]
    greet([{"seq": lax.rem(me + d, count)} for d in range(1, count)])

    def advance(t, states):
        step = step_ref[t]
        drive = step * inner_ref[t]
        return step, tuple(
            jnp.exp(step * rate_ref[n]) * states[n] + maps_ref[t, n] * drive for n in range(STATE)
        )

    def ending(t, carried):
        states, total = carried
        step, states = advance(t, states)
        return states, total + step

    zero = jnp.zeros(tile, F32)
    states, total = lax.fori_loop(0, tokens, ending, ((zero,) * STATE, zero))
    for n in range(STATE):
        outgoing[n] = states[n].astype(BF16)
    upper = total.astype(BF16)
    outgoing[STATE] = upper
    outgoing[STATE + 1] = (total - upper.astype(F32)).astype(BF16)

    def copy_by(d):
        return send(
            outgoing,
            arriving.at[d],
            send_sems.at[d],
            recv_sems.at[d],
            {"seq": lax.rem(me + d, count)},
        )

    for d in range(1, count):

        @pl.when(me + d < count)
        def _():
            copy_by(d).start()

    state[...] = jnp.zeros(state.shape, F32)
    for d in range(count - 1, 0, -1):

        @pl.when(me >= d)
        def _():
            copy_by(d).wait_recv()
            passed = arriving[d, STATE].astype(F32) + arriving[d, STATE + 1].astype(F32)
            for n in range(STATE):
                state[n] = jnp.exp(passed * rate_ref[n]) * state[n] + arriving[d, n].astype(F32)

    def reading(t, states):
        _, states = advance(t, states)
        terms = [maps_ref[t, STATE + n] * states[n] for n in range(STATE)]
        while len(terms) > 1:
            terms = [a + b for a, b in zip(terms[::2], terms[1::2])]
        out_ref[t] = terms[0]
        return states

    lax.fori_loop(0, tokens, reading, tuple(state[n] for n in range(STATE)))
    for d in range(1, count):

        @pl.when(me + d < count)
        def _():
            copy_by(d).wait_send()


def recur(step_size, inner, maps, decay_rate):
    count = lax.axis_size("seq")
    tokens, channels = step_size.shape
    tile = (channels // 128, 128)
    rate = -decay_rate.T.reshape(STATE, *tile)
    out = pl.pallas_call(
        functools.partial(scan_kernel, count),
        out_shape=jax.ShapeDtypeStruct((tokens, *tile), F32),
        in_specs=[VMEM_SPEC, VMEM_SPEC, SMEM_SPEC, VMEM_SPEC],
        out_specs=VMEM_SPEC,
        scratch_shapes=[
            pltpu.VMEM((STATE, *tile), F32),
            pltpu.VMEM((STATE + 2, *tile), BF16),
            pltpu.VMEM((count, STATE + 2, *tile), BF16),
            pltpu.SemaphoreType.DMA((count,)),
            pltpu.SemaphoreType.DMA((count,)),
        ],
        compiler_params=pltpu.CompilerParams(
            collective_id=1, has_side_effects=True, vmem_limit_bytes=24 * MIB
        ),
        name="recurrence",
    )(step_size.reshape(tokens, *tile), inner.reshape(tokens, *tile), maps, rate)
    return out.reshape(tokens, channels)


def mixer_kernel(count, part_ref, residual_ref, gain_ref, mixer_ref, normed_ref, *scratch):
    stages = stages_of(count)
    works, arrivings = scratch[:stages], scratch[stages : 2 * stages]
    columns, send_sems, recv_sems, gather_send_sems, gather_recv_sems = scratch[2 * stages :]
    me = lax.axis_index("tp")
    greet([{"tp": lax.rem(me + d, count)} for d in range(1, count)])
    total = None
    for k in range(stages):
        source = part_ref if k == 0 else works[k]
        kept = count // 2 ** (k + 1)
        bit = bit_of(me, k)
        copies = [
            send(
                source.at[2 * i + 1 - bit],
                arrivings[k].at[i],
                send_sems.at[k, i],
                recv_sems.at[k, i],
                {"tp": flipped(me, k)},
            )
            for i in range(kept)
        ]
        for copy in copies:
            copy.start()
        for i, copy in enumerate(copies):
            copy.wait()
            total = source[2 * i + bit].astype(F32) + arrivings[k][i].astype(F32)
            if k < stages - 1:
                works[k + 1][i] = total.astype(BF16)
    mixer = (total + residual_ref[...].astype(F32)).astype(BF16)
    mixer_ref[...] = mixer
    wide = mixer.astype(F32)
    normed = (
        wide * lax.rsqrt(jnp.mean(wide * wide, axis=1, keepdims=True) + 1e-06) * gain_ref[...]
    ).astype(BF16)
    part_width = columns.shape[2]
    for j in range(count):
        columns[j] = normed[:, j * part_width : (j + 1) * part_width]
    copies = []
    for d in range(1, count):
        peer = lax.rem(me + d, count)
        copies.append(
            send(
                columns.at[peer],
                normed_ref.at[me],
                gather_send_sems.at[d],
                gather_recv_sems.at[d],
                {"tp": peer},
            )
        )
    for copy in copies:
        copy.start()
    normed_ref[me] = columns[me]
    for copy in copies:
        copy.wait()


def mixer_rows(part, residual, gain):
    count = lax.axis_size("tp")
    stages = stages_of(count)
    rows, width = residual.shape
    sems = pltpu.SemaphoreType.DMA((stages, count // 2))
    return pl.pallas_call(
        functools.partial(mixer_kernel, count),
        out_shape=(
            jax.ShapeDtypeStruct((rows, width), BF16),
            jax.ShapeDtypeStruct((count, rows, width // count), BF16),
        ),
        in_specs=[VMEM_SPEC] * 3,
        out_specs=(VMEM_SPEC, VMEM_SPEC),
        scratch_shapes=[pltpu.VMEM((count // 2**k, rows, width), BF16) for k in range(stages)]
        + [pltpu.VMEM((count // 2 ** (k + 1), rows, width), BF16) for k in range(stages)]
        + [pltpu.VMEM((count, rows, width // count), BF16)]
        + [sems] * 2
        + [pltpu.SemaphoreType.DMA((count,))] * 2,
        compiler_params=pltpu.CompilerParams(
            collective_id=2, has_side_effects=True, vmem_limit_bytes=32 * MIB
        ),
        name="mixer_sum",
    )(part.reshape(count, rows, width), residual, gain.reshape(1, width))


def dispatch_kernel(
    count,
    lanes,
    group,
    placing_ref,
    normed_ref,
    out_ref,
    slots,
    send_sems,
    recv_sems,
    spread_send_sems,
    spread_recv_sems,
):
    me, lane = lax.axis_index("seq"), lax.axis_index("tp")
    stages = stages_of(lanes)
    capacity, part_width = slots.shape[1:]
    greet(
        [{"seq": lax.rem(me + d, count)} for d in range(1, count)]
        + [{"tp": flipped(lane, k)} for k in range(stages)]
    )

    def block(source, column):
        return (
            pl.ds(pl.multiple_of(source * capacity, 16), capacity),
            pl.ds(pl.multiple_of(column * part_width, 128), part_width),
        )

    placed = jnp.dot(placing_ref[...], normed_ref[...], preferred_element_type=F32).astype(BF16)
    for e in range(EXPERTS):
        slots[e] = placed[e * capacity : (e + 1) * capacity]
    firsts = []
    for d in range(1, count):
        target = lax.rem(me + d, count)
        firsts.append(
            send(
                slots.at[target // group],
                out_ref.at[block(me, lane)],
                send_sems.at[d],
                recv_sems.at[d],
                {"seq": target},
            )
        )
        firsts[-1].start()
    out_ref[block(me, lane)] = slots[me // group]

    spread = {}
    for step in range(count + stages - 1):
        for k in range(stages - 1, -1, -1):
            d = step - (stages - 1 - k)
            if d < 0 or d >= count:
                continue
            if k == stages - 1:
                if d > 0:
                    firsts[d - 1].wait_recv()
            else:
                for copy in spread[d, k + 1]:
                    copy.wait_recv()
            source = lax.rem(me - d + count, count)
            low = lax.rem(lane, 2 ** (k + 1))
            spread[d, k] = []
            for i in range(lanes // 2 ** (k + 1)):
                place = out_ref.at[block(source, low + 2 ** (k + 1) * i)]
                copy = send(
                    place,
                    place,
                    spread_send_sems.at[d, k, i],
                    spread_recv_sems.at[d, k, i],
                    {"tp": flipped(lane, k)},
                )
                copy.start()
                spread[d, k].append(copy)
    for copy in firsts:
        copy.wait_send()
    for (_, k), copies in spread.items():
        for copy in copies:
            copy.wait_send()
            if k == 0:
                copy.wait_recv()


def dispatch(placing, normed, group):
    count, lanes = lax.axis_size("seq"), lax.axis_size("tp")
    stages = stages_of(lanes)
    capacity = placing.shape[0] // EXPERTS
    part_width = normed.shape[1]
    return pl.pallas_call(
        functools.partial(dispatch_kernel, count, lanes, group),
        out_shape=jax.ShapeDtypeStruct((count * capacity, lanes * part_width), BF16),
        in_specs=[VMEM_SPEC] * 2,
        out_specs=VMEM_SPEC,
        scratch_shapes=[pltpu.VMEM((EXPERTS, capacity, part_width), BF16)]
        + [pltpu.SemaphoreType.DMA((count,))] * 2
        + [pltpu.SemaphoreType.DMA((count, stages, lanes // 2))] * 2,
        compiler_params=pltpu.CompilerParams(
            collective_id=3, has_side_effects=True, vmem_limit_bytes=32 * MIB
        ),
        name="dispatch",
    )(placing, normed)


def return_kernel(
    count, lanes, part_ref, pick_ref, prob_ref, mixer_ref, out_ref, *scratch
):
    stages = stages_of(lanes)
    works, arrivings = scratch[:stages], scratch[stages : 2 * stages]
    home, outgoing, incoming = scratch[2 * stages : 2 * stages + 3]
    sum_send, sum_recv, home_send, home_recv, row_send, row_recv = scratch[2 * stages + 3 :]
    me, lane = lax.axis_index("seq"), lax.axis_index("tp")
    capacity, part_width = home.shape[1:]
    greet(
        [{"seq": lax.rem(me + d, count)} for d in range(1, count)]
        + [{"tp": lax.rem(lane + d, lanes)} for d in range(1, lanes)]
    )

    def block(d, column):
        target = lax.rem(me + d, count)
        return (
            pl.ds(pl.multiple_of(target * capacity, 16), capacity),
            pl.ds(pl.multiple_of(column * part_width, 128), part_width),
        )

    def start(d, k):
        bit = bit_of(lane, k)
        copies = []
        for i in range(lanes // 2 ** (k + 1)):
            index = 2 * i + 1 - bit
            source = part_ref.at[block(d, index)] if k == 0 else works[k - 1].at[d, index]
            copy = send(
                source,
                arrivings[k].at[d, i],
                sum_send.at[d, k, i],
                sum_recv.at[d, k, i],
                {"tp": flipped(lane, k)},
            )
            copy.start()
            copies.append(copy)
        return copies

    def finish(d, k, copies):
        bit = bit_of(lane, k)
        for i, copy in enumerate(copies):
            copy.wait_recv()
            index = 2 * i + bit
            mine = part_ref[block(d, index)] if k == 0 else works[k - 1][d, index]
            works[k][d, i] = (mine.astype(F32) + arrivings[k][d, i].astype(F32)).astype(BF16)

    order = list(range(1, count)) + [0]
    sums = {(d, 0): start(d, 0) for d in order}
    homes = []
    for step in range(count + stages - 1):
        for k in range(stages):
            if step - k < 0 or step - k >= count:
                continue
            d = order[step - k]
            finish(d, k, sums[d, k])
            if k < stages - 1:
                sums[d, k + 1] = start(d, k + 1)
            elif d == 0:
                home[me] = works[k][0, 0]
            else:
                copy = send(
                    works[k].at[d, 0],
                    home.at[me],
                    home_send.at[d],
                    home_recv.at[d],
                    {"seq": lax.rem(me + d, count)},
                )
                copy.start()
                homes.append(copy)
    for copy in homes:
        copy.wait_recv()
    arrived = home[...].reshape(count * capacity, part_width)
    picked = jnp.dot(pick_ref[...], arrived, preferred_element_type=F32) * prob_ref[...]
    half = picked.shape[0] // 2
    outgoing[...] = (picked[:half] + picked[half:]).astype(BF16).reshape(outgoing.shape)
    rows = []
    for d in range(1, lanes):
        peer = lax.rem(lane + d, lanes)
        copy = send(
            outgoing.at[peer], incoming.at[lane], row_send.at[d], row_recv.at[d], {"tp": peer}
        )
        copy.start()
        rows.append(copy)
    incoming[lane] = outgoing[lane]
    for copy in rows:
        copy.wait()
    for j in range(lanes):
        span = slice(j * part_width, (j + 1) * part_width)
        out_ref[:, span] = (mixer_ref[:, span].astype(F32) + incoming[j].astype(F32)).astype(BF16)
    for copy in homes:
        copy.wait_send()
    for copies in sums.values():
        for copy in copies:
            copy.wait_send()


def bring_back(part, pick, prob, mixer):
    count, lanes = lax.axis_size("seq"), lax.axis_size("tp")
    stages = stages_of(lanes)
    rows, width = mixer.shape
    block = (part.shape[0] // count, width // lanes)
    sums = [
        pltpu.VMEM((count, lanes // 2 ** (k + 1), *block), BF16) for _ in range(2) for k in range(stages)
    ]
    return pl.pallas_call(
        functools.partial(return_kernel, count, lanes),
        out_shape=jax.ShapeDtypeStruct((rows, width), BF16),
        in_specs=[VMEM_SPEC] * 4,
        out_specs=VMEM_SPEC,
        scratch_shapes=sums
        + [pltpu.VMEM((count, *block), BF16)]
        + [pltpu.VMEM((lanes, rows, block[1]), BF16)] * 2
        + [pltpu.SemaphoreType.DMA((count, stages, lanes // 2))] * 2
        + [pltpu.SemaphoreType.DMA((count,))] * 2
        + [pltpu.SemaphoreType.DMA((lanes,))] * 2,
        compiler_params=pltpu.CompilerParams(
            collective_id=4, has_side_effects=True, vmem_limit_bytes=40 * MIB
        ),
        name="bring_back",
    )(part, pick, prob, mixer)


def expert_share(arrived_flat, up_weight, down_weight):
    hidden = jax.nn.silu(jnp.dot(arrived_flat, up_weight, preferred_element_type=F32)).astype(BF16)
    return jnp.dot(hidden, down_weight, preferred_element_type=F32).astype(BF16)


def routing(expert_ids, gate_prob):
    rows = expert_ids.shape[0]
    lanes = lax.axis_size("tp")
    capacity = 3 * rows // EXPERTS
    both = lax.all_gather(
        jnp.concatenate([expert_ids.astype(F32), gate_prob], axis=1), "tp", axis=0
    )
    chosen = both[:, :, :2].astype(jnp.int32).reshape(lanes, rows * 2)
    hits = (chosen[:, :, None] == jnp.arange(EXPERTS, dtype=jnp.int32)).astype(jnp.int32)
    earlier = jnp.cumsum(hits, axis=1) - hits
    slot = jnp.sum(earlier * hits, axis=2)
    source = jnp.arange(lanes, dtype=jnp.int32)[:, None]
    target = (chosen * lanes + source) * capacity + slot
    return target.reshape(lanes * rows, 2), both[:, :, 2:].reshape(lanes * rows, 2)


def per_device(
    x_in,
    gate_in,
    conv_weight,
    conv_bias,
    x_weight,
    dt_weight,
    dt_bias,
    decay_rate,
    skip_gain,
    out_weight,
    residual_in,
    norm_gain,
    expert_ids,
    gate_prob,
    up_weight,
    down_weight,
):
    tokens, channels = x_in.shape
    route = routing(expert_ids, gate_prob)
    width = out_weight.shape[1]
    reach = conv_weight.shape[0] - 1
    rim_rows = shifted(x_in[tokens - reach :], "seq", 1)
    padded = jnp.concatenate([rim_rows, x_in], axis=0).astype(F32)
    conv_out = conv_bias[None, :] + sum(
        (
            conv_weight[offset][None, :] * padded[offset : offset + tokens]
            for offset in range(reach + 1)
        )
    )
    inner = jax.nn.silu(conv_out).astype(BF16)
    projected = sum_over_tp(jnp.dot(inner, x_weight, preferred_element_type=F32).astype(BF16))
    dt_low = projected[:, :DTRANK].astype(BF16)
    step_size = jax.nn.softplus(
        jnp.dot(dt_low, dt_weight, preferred_element_type=F32) + dt_bias[None, :]
    )
    ssm = recur(step_size, inner.astype(F32), projected[:, DTRANK:], decay_rate)
    mixed = (
        (ssm + skip_gain[None, :] * inner.astype(F32)) * jax.nn.silu(gate_in.astype(F32))
    ).astype(BF16)
    rows = tokens // lax.axis_size("tp")
    mixer_out, normed_part = mixer_rows(
        jnp.dot(mixed, out_weight, preferred_element_type=F32).astype(BF16), residual_in, norm_gain
    )
    count, lanes = lax.axis_size("seq"), lax.axis_size("tp")
    group = count // EXPERTS
    capacity = 3 * rows // EXPERTS
    spread = lanes * capacity
    target, prob = route
    placing = jnp.sum(
        (jnp.arange(EXPERTS * spread, dtype=jnp.int32)[:, None, None] == target[None]).astype(BF16),
        axis=2,
    )
    column = jnp.arange(count * spread, dtype=jnp.int32)
    column = column // (spread * group) * spread + column % spread
    pick = (target.T.reshape(-1)[:, None] == column[None, :]).astype(BF16)
    arrived = dispatch(placing, normed_part.reshape(tokens, width // lanes), group)
    share = expert_share(arrived, up_weight, down_weight)
    return (mixer_out, bring_back(share, pick, prob.T.reshape(-1, 1), mixer_out))


def solution(mesh):
    return jax.shard_map(
        per_device,
        mesh=mesh,
        in_specs=(
            P("seq", "tp"),
            P("seq", "tp"),
            P(None, "tp"),
            P("tp"),
            P("tp", None),
            P(None, "tp"),
            P("tp"),
            P("tp", None),
            P("tp"),
            P("tp", None),
            P(("seq", "tp"), None),
            P(),
            P(("seq", "tp"), None),
            P(("seq", "tp"), None),
            P(None, ("seq", "tp")),
            P(("seq", "tp"), None),
        ),
        out_specs=(P(("seq", "tp"), None), P(("seq", "tp"), None)),
        check_vma=False,
    )
```

```python
import functools

import jax
import jax.numpy as jnp
from jax import lax
from jax.experimental import pallas as pl
from jax.experimental.pallas import tpu as pltpu
from jax.sharding import PartitionSpec as P

STATE = 16
DTRANK = 512
EXPERTS = 8
MESH = pl.DeviceIdType.MESH
VMEM_SPEC = pl.BlockSpec(memory_space=pltpu.VMEM)
SMEM_SPEC = pl.BlockSpec(memory_space=pltpu.SMEM)
F32 = jnp.float32
BF16 = jnp.bfloat16
MIB = 1024 * 1024
AHEAD = 3
LAG = 2


def shifted(value, axis, steps):
    count = lax.axis_size(axis)
    initial, last = (max(0, -steps), min(count, count - steps))
    return lax.ppermute(value, axis, [(source, source + steps) for source in range(initial, last)])


def greet(peers):
    barrier = pltpu.get_barrier_semaphore()
    for peer in peers:
        pl.semaphore_signal(barrier, inc=1, device_id=peer, device_id_type=MESH)
    pl.semaphore_wait(barrier, len(peers))


def send(source, target, send_sem, recv_sem, device):
    return pltpu.make_async_remote_copy(
        src_ref=source,
        dst_ref=target,
        send_sem=send_sem,
        recv_sem=recv_sem,
        device_id=device,
        device_id_type=MESH,
    )


def bit_of(index, stage):
    return lax.rem(index // 2**stage, 2)


def flipped(index, stage):
    return index + 2**stage - 2 * 2**stage * bit_of(index, stage)


def stages_of(count):
    return count.bit_length() - 1


def sum_kernel(
    count,
    part_ref,
    route_ref,
    out_ref,
    routes_ref,
    outgoing,
    arriving,
    send_sems,
    recv_sems,
    route_send_sems,
    route_recv_sems,
):
    me = lax.axis_index("tp")
    stages = stages_of(count)
    greet([{"tp": lax.rem(me + d, count)} for d in range(1, count)])
    routes = [
        send(
            route_ref,
            routes_ref.at[me],
            route_send_sems.at[d],
            route_recv_sems.at[d],
            {"tp": lax.rem(me + d, count)},
        )
        for d in range(1, count)
    ]
    for k in range(stages):
        source = part_ref if k == 0 else outgoing
        copy = send(
            source, arriving.at[k], send_sems.at[k], recv_sems.at[k], {"tp": flipped(me, k)}
        )
        copy.start()
        if k == 0:
            for route in routes:
                route.start()
            routes_ref[me] = route_ref[...]
        copy.wait()
        total = source[...].astype(F32) + arriving[k].astype(F32)
        if k < stages - 1:
            outgoing[...] = total.astype(BF16)
        else:
            out_ref[...] = total
    for route in routes:
        route.wait()


def sum_over_tp(part, route):
    count = lax.axis_size("tp")
    stages = stages_of(count)
    return pl.pallas_call(
        functools.partial(sum_kernel, count),
        out_shape=(
            jax.ShapeDtypeStruct(part.shape, F32),
            jax.ShapeDtypeStruct((count, *route.shape), F32),
        ),
        in_specs=[VMEM_SPEC] * 2,
        out_specs=(VMEM_SPEC, VMEM_SPEC),
        scratch_shapes=[
            pltpu.VMEM(part.shape, BF16),
            pltpu.VMEM((stages, *part.shape), BF16),
            pltpu.SemaphoreType.DMA((stages,)),
            pltpu.SemaphoreType.DMA((stages,)),
            pltpu.SemaphoreType.DMA((count,)),
            pltpu.SemaphoreType.DMA((count,)),
        ],
        compiler_params=pltpu.CompilerParams(collective_id=0, has_side_effects=True),
        name="projection_sum",
    )(part, route)


def scan_kernel(
    count,
    step_ref,
    inner_ref,
    maps_ref,
    rate_ref,
    out_ref,
    state,
    outgoing,
    arriving,
    send_sems,
    recv_sems,
):
    me = lax.axis_index("seq")
    tokens = step_ref.shape[0]
    tile = step_ref.shape[1:]
    greet([{"seq": lax.rem(me + d, count)} for d in range(1, count)])

    def advance(t, states):
        step = step_ref[t]
        drive = step * inner_ref[t]
        return step, tuple(
            jnp.exp(step * rate_ref[n]) * states[n] + maps_ref[t, n] * drive for n in range(STATE)
        )

    def ending(t, carried):
        states, total = carried
        step, states = advance(t, states)
        return states, total + step

    zero = jnp.zeros(tile, F32)
    states, total = lax.fori_loop(0, tokens, ending, ((zero,) * STATE, zero))
    for n in range(STATE):
        outgoing[n] = states[n].astype(BF16)
    upper = total.astype(BF16)
    outgoing[STATE] = upper
    outgoing[STATE + 1] = (total - upper.astype(F32)).astype(BF16)

    def copy_by(d):
        return send(
            outgoing,
            arriving.at[d],
            send_sems.at[d],
            recv_sems.at[d],
            {"seq": lax.rem(me + d, count)},
        )

    for d in range(1, count):

        @pl.when(me + d < count)
        def _():
            copy_by(d).start()

    state[...] = jnp.zeros(state.shape, F32)
    for d in range(count - 1, 0, -1):

        @pl.when(me >= d)
        def _():
            copy_by(d).wait_recv()
            passed = arriving[d, STATE].astype(F32) + arriving[d, STATE + 1].astype(F32)
            for n in range(STATE):
                state[n] = jnp.exp(passed * rate_ref[n]) * state[n] + arriving[d, n].astype(F32)

    def reading(t, states):
        _, states = advance(t, states)
        terms = [maps_ref[t, STATE + n] * states[n] for n in range(STATE)]
        while len(terms) > 1:
            terms = [a + b for a, b in zip(terms[::2], terms[1::2])]
        out_ref[t] = terms[0]
        return states

    lax.fori_loop(0, tokens, reading, tuple(state[n] for n in range(STATE)))
    for d in range(1, count):

        @pl.when(me + d < count)
        def _():
            copy_by(d).wait_send()


def recur(step_size, inner, maps, decay_rate):
    count = lax.axis_size("seq")
    tokens, channels = step_size.shape
    tile = (channels // 128, 128)
    rate = -decay_rate.T.reshape(STATE, *tile)
    out = pl.pallas_call(
        functools.partial(scan_kernel, count),
        out_shape=jax.ShapeDtypeStruct((tokens, *tile), F32),
        in_specs=[VMEM_SPEC, VMEM_SPEC, SMEM_SPEC, VMEM_SPEC],
        out_specs=VMEM_SPEC,
        scratch_shapes=[
            pltpu.VMEM((STATE, *tile), F32),
            pltpu.VMEM((STATE + 2, *tile), BF16),
            pltpu.VMEM((count, STATE + 2, *tile), BF16),
            pltpu.SemaphoreType.DMA((count,)),
            pltpu.SemaphoreType.DMA((count,)),
        ],
        compiler_params=pltpu.CompilerParams(
            collective_id=1, has_side_effects=True, vmem_limit_bytes=24 * MIB
        ),
        name="recurrence",
    )(step_size.reshape(tokens, *tile), inner.reshape(tokens, *tile), maps, rate)
    return out.reshape(tokens, channels)


def mixer_kernel(count, part_ref, residual_ref, gain_ref, mixer_ref, normed_ref, *scratch):
    stages = stages_of(count)
    works, arrivings = scratch[:stages], scratch[stages : 2 * stages]
    columns, send_sems, recv_sems, gather_send_sems, gather_recv_sems = scratch[2 * stages :]
    me = lax.axis_index("tp")
    greet([{"tp": lax.rem(me + d, count)} for d in range(1, count)])
    total = None
    for k in range(stages):
        source = part_ref if k == 0 else works[k]
        kept = count // 2 ** (k + 1)
        bit = bit_of(me, k)
        copies = [
            send(
                source.at[2 * i + 1 - bit],
                arrivings[k].at[i],
                send_sems.at[k, i],
                recv_sems.at[k, i],
                {"tp": flipped(me, k)},
            )
            for i in range(kept)
        ]
        for copy in copies:
            copy.start()
        for i, copy in enumerate(copies):
            copy.wait()
            total = source[2 * i + bit].astype(F32) + arrivings[k][i].astype(F32)
            if k < stages - 1:
                works[k + 1][i] = total.astype(BF16)
    mixer = (total + residual_ref[...].astype(F32)).astype(BF16)
    mixer_ref[...] = mixer
    wide = mixer.astype(F32)
    normed = (
        wide * lax.rsqrt(jnp.mean(wide * wide, axis=1, keepdims=True) + 1e-06) * gain_ref[...]
    ).astype(BF16)
    part_width = columns.shape[2]
    for j in range(count):
        columns[j] = normed[:, j * part_width : (j + 1) * part_width]
    copies = []
    for d in range(1, count):
        peer = lax.rem(me + d, count)
        copies.append(
            send(
                columns.at[peer],
                normed_ref.at[me],
                gather_send_sems.at[d],
                gather_recv_sems.at[d],
                {"tp": peer},
            )
        )
    for copy in copies:
        copy.start()
    normed_ref[me] = columns[me]
    for copy in copies:
        copy.wait()


def mixer_rows(part, residual, gain):
    count = lax.axis_size("tp")
    stages = stages_of(count)
    rows, width = residual.shape
    sems = pltpu.SemaphoreType.DMA((stages, count // 2))
    return pl.pallas_call(
        functools.partial(mixer_kernel, count),
        out_shape=(
            jax.ShapeDtypeStruct((rows, width), BF16),
            jax.ShapeDtypeStruct((count, rows, width // count), BF16),
        ),
        in_specs=[VMEM_SPEC] * 3,
        out_specs=(VMEM_SPEC, VMEM_SPEC),
        scratch_shapes=[pltpu.VMEM((count // 2**k, rows, width), BF16) for k in range(stages)]
        + [pltpu.VMEM((count // 2 ** (k + 1), rows, width), BF16) for k in range(stages)]
        + [pltpu.VMEM((count, rows, width // count), BF16)]
        + [sems] * 2
        + [pltpu.SemaphoreType.DMA((count,))] * 2,
        compiler_params=pltpu.CompilerParams(
            collective_id=2, has_side_effects=True, vmem_limit_bytes=32 * MIB
        ),
        name="mixer_sum",
    )(part.reshape(count, rows, width), residual, gain.reshape(1, width))


def dispatch_kernel(
    count,
    lanes,
    group,
    placing_ref,
    normed_ref,
    out_ref,
    slots,
    send_sems,
    recv_sems,
    spread_send_sems,
    spread_recv_sems,
):
    me, lane = lax.axis_index("seq"), lax.axis_index("tp")
    stages = stages_of(lanes)
    capacity, part_width = slots.shape[1:]
    greet(
        [{"seq": lax.rem(me + d, count)} for d in range(1, count)]
        + [{"tp": flipped(lane, k)} for k in range(stages)]
    )

    def block(source, column):
        return (
            pl.ds(pl.multiple_of(source * capacity, 16), capacity),
            pl.ds(pl.multiple_of(column * part_width, 128), part_width),
        )

    placed = jnp.dot(placing_ref[...], normed_ref[...], preferred_element_type=F32).astype(BF16)
    for e in range(EXPERTS):
        slots[e] = placed[e * capacity : (e + 1) * capacity]
    firsts = []
    for d in range(1, count):
        target = lax.rem(me + d, count)
        firsts.append(
            send(
                slots.at[target // group],
                out_ref.at[block(me, lane)],
                send_sems.at[d],
                recv_sems.at[d],
                {"seq": target},
            )
        )
        if d <= AHEAD:
            firsts[-1].start()
    out_ref[block(me, lane)] = slots[me // group]

    spread = {}
    for step in range(count + LAG * (stages - 1)):
        for k in range(stages - 1, -1, -1):
            d = step - LAG * (stages - 1 - k)
            if d < 0 or d >= count:
                continue
            if k == stages - 1:
                if d > 0:
                    firsts[d - 1].wait_recv()
                    if d + AHEAD < count:
                        firsts[d - 1 + AHEAD].start()
            else:
                for copy in spread[d, k + 1]:
                    copy.wait_recv()
            source = lax.rem(me - d + count, count)
            low = lax.rem(lane, 2 ** (k + 1))
            spread[d, k] = []
            for i in range(lanes // 2 ** (k + 1)):
                place = out_ref.at[block(source, low + 2 ** (k + 1) * i)]
                copy = send(
                    place,
                    place,
                    spread_send_sems.at[d, k, i],
                    spread_recv_sems.at[d, k, i],
                    {"tp": flipped(lane, k)},
                )
                copy.start()
                spread[d, k].append(copy)
    for copy in firsts:
        copy.wait_send()
    for (_, k), copies in spread.items():
        for copy in copies:
            copy.wait_send()
            if k == 0:
                copy.wait_recv()


def dispatch(placing, normed, group):
    count, lanes = lax.axis_size("seq"), lax.axis_size("tp")
    stages = stages_of(lanes)
    capacity = placing.shape[0] // EXPERTS
    part_width = normed.shape[1]
    return pl.pallas_call(
        functools.partial(dispatch_kernel, count, lanes, group),
        out_shape=jax.ShapeDtypeStruct((count * capacity, lanes * part_width), BF16),
        in_specs=[VMEM_SPEC] * 2,
        out_specs=VMEM_SPEC,
        scratch_shapes=[pltpu.VMEM((EXPERTS, capacity, part_width), BF16)]
        + [pltpu.SemaphoreType.DMA((count,))] * 2
        + [pltpu.SemaphoreType.DMA((count, stages, lanes // 2))] * 2,
        compiler_params=pltpu.CompilerParams(
            collective_id=3, has_side_effects=True, vmem_limit_bytes=32 * MIB
        ),
        name="dispatch",
    )(placing, normed)


def return_kernel(
    count, lanes, part_ref, pick_ref, prob_ref, mixer_ref, out_ref, *scratch
):
    stages = stages_of(lanes)
    works, arrivings = scratch[:stages], scratch[stages : 2 * stages]
    home, outgoing, incoming = scratch[2 * stages : 2 * stages + 3]
    sum_send, sum_recv, home_send, home_recv, row_send, row_recv = scratch[2 * stages + 3 :]
    me, lane = lax.axis_index("seq"), lax.axis_index("tp")
    capacity, part_width = home.shape[1:]
    greet(
        [{"seq": lax.rem(me + d, count)} for d in range(1, count)]
        + [{"tp": lax.rem(lane + d, lanes)} for d in range(1, lanes)]
    )

    def block(d, column):
        target = lax.rem(me + d, count)
        return (
            pl.ds(pl.multiple_of(target * capacity, 16), capacity),
            pl.ds(pl.multiple_of(column * part_width, 128), part_width),
        )

    def start(d, k):
        bit = bit_of(lane, k)
        copies = []
        for i in range(lanes // 2 ** (k + 1)):
            index = 2 * i + 1 - bit
            source = part_ref.at[block(d, index)] if k == 0 else works[k - 1].at[d, index]
            copy = send(
                source,
                arrivings[k].at[d, i],
                sum_send.at[d, k, i],
                sum_recv.at[d, k, i],
                {"tp": flipped(lane, k)},
            )
            copy.start()
            copies.append(copy)
        return copies

    def finish(d, k, copies):
        bit = bit_of(lane, k)
        for i, copy in enumerate(copies):
            copy.wait_recv()
            index = 2 * i + bit
            mine = part_ref[block(d, index)] if k == 0 else works[k - 1][d, index]
            works[k][d, i] = (mine.astype(F32) + arrivings[k][d, i].astype(F32)).astype(BF16)

    order = list(range(1, count)) + [0]
    sums = {(d, 0): start(d, 0) for d in order}
    homes = []
    for step in range(count + LAG * (stages - 1)):
        for k in range(stages):
            if step - LAG * k < 0 or step - LAG * k >= count:
                continue
            d = order[step - LAG * k]
            finish(d, k, sums[d, k])
            if k < stages - 1:
                sums[d, k + 1] = start(d, k + 1)
            elif d == 0:
                home[me] = works[k][0, 0]
            else:
                copy = send(
                    works[k].at[d, 0],
                    home.at[me],
                    home_send.at[d],
                    home_recv.at[d],
                    {"seq": lax.rem(me + d, count)},
                )
                copy.start()
                homes.append(copy)
    for copy in homes:
        copy.wait_recv()
    arrived = home[...].reshape(count * capacity, part_width)
    picked = jnp.dot(pick_ref[...], arrived, preferred_element_type=F32) * prob_ref[...]
    half = picked.shape[0] // 2
    outgoing[...] = (picked[:half] + picked[half:]).astype(BF16).reshape(outgoing.shape)
    rows = []
    for d in range(1, lanes):
        peer = lax.rem(lane + d, lanes)
        copy = send(
            outgoing.at[peer], incoming.at[lane], row_send.at[d], row_recv.at[d], {"tp": peer}
        )
        copy.start()
        rows.append(copy)
    incoming[lane] = outgoing[lane]
    for copy in rows:
        copy.wait()
    for j in range(lanes):
        span = slice(j * part_width, (j + 1) * part_width)
        out_ref[:, span] = (mixer_ref[:, span].astype(F32) + incoming[j].astype(F32)).astype(BF16)
    for copy in homes:
        copy.wait_send()
    for copies in sums.values():
        for copy in copies:
            copy.wait_send()


def bring_back(part, pick, prob, mixer):
    count, lanes = lax.axis_size("seq"), lax.axis_size("tp")
    stages = stages_of(lanes)
    rows, width = mixer.shape
    block = (part.shape[0] // count, width // lanes)
    sums = [
        pltpu.VMEM((count, lanes // 2 ** (k + 1), *block), BF16) for _ in range(2) for k in range(stages)
    ]
    return pl.pallas_call(
        functools.partial(return_kernel, count, lanes),
        out_shape=jax.ShapeDtypeStruct((rows, width), BF16),
        in_specs=[VMEM_SPEC] * 4,
        out_specs=VMEM_SPEC,
        scratch_shapes=sums
        + [pltpu.VMEM((count, *block), BF16)]
        + [pltpu.VMEM((lanes, rows, block[1]), BF16)] * 2
        + [pltpu.SemaphoreType.DMA((count, stages, lanes // 2))] * 2
        + [pltpu.SemaphoreType.DMA((count,))] * 2
        + [pltpu.SemaphoreType.DMA((lanes,))] * 2,
        compiler_params=pltpu.CompilerParams(
            collective_id=4, has_side_effects=True, vmem_limit_bytes=40 * MIB
        ),
        name="bring_back",
    )(part, pick, prob, mixer)


def expert_share(arrived_flat, up_weight, down_weight):
    hidden = jax.nn.silu(jnp.dot(arrived_flat, up_weight, preferred_element_type=F32)).astype(BF16)
    return jnp.dot(hidden, down_weight, preferred_element_type=F32).astype(BF16)


def routing(both):
    lanes, rows = both.shape[:2]
    capacity = 3 * rows // EXPERTS
    chosen = both[:, :, :2].astype(jnp.int32).reshape(lanes, rows * 2)
    hits = (chosen[:, :, None] == jnp.arange(EXPERTS, dtype=jnp.int32)).astype(jnp.int32)
    earlier = jnp.cumsum(hits, axis=1) - hits
    slot = jnp.sum(earlier * hits, axis=2)
    source = jnp.arange(lanes, dtype=jnp.int32)[:, None]
    target = (chosen * lanes + source) * capacity + slot
    return target.reshape(lanes * rows, 2), both[:, :, 2:].reshape(lanes * rows, 2)


def per_device(
    x_in,
    gate_in,
    conv_weight,
    conv_bias,
    x_weight,
    dt_weight,
    dt_bias,
    decay_rate,
    skip_gain,
    out_weight,
    residual_in,
    norm_gain,
    expert_ids,
    gate_prob,
    up_weight,
    down_weight,
):
    tokens, channels = x_in.shape
    width = out_weight.shape[1]
    reach = conv_weight.shape[0] - 1
    rim_rows = shifted(x_in[tokens - reach :], "seq", 1)
    padded = jnp.concatenate([rim_rows, x_in], axis=0).astype(F32)
    conv_out = conv_bias[None, :] + sum(
        (
            conv_weight[offset][None, :] * padded[offset : offset + tokens]
            for offset in range(reach + 1)
        )
    )
    inner = jax.nn.silu(conv_out).astype(BF16)
    projected, both = sum_over_tp(
        jnp.dot(inner, x_weight, preferred_element_type=F32).astype(BF16),
        jnp.concatenate([expert_ids.astype(F32), gate_prob], axis=1),
    )
    dt_low = projected[:, :DTRANK].astype(BF16)
    step_size = jax.nn.softplus(
        jnp.dot(dt_low, dt_weight, preferred_element_type=F32) + dt_bias[None, :]
    )
    ssm = recur(step_size, inner.astype(F32), projected[:, DTRANK:], decay_rate)
    mixed = (
        (ssm + skip_gain[None, :] * inner.astype(F32)) * jax.nn.silu(gate_in.astype(F32))
    ).astype(BF16)
    rows = tokens // lax.axis_size("tp")
    mixer_out, normed_part = mixer_rows(
        jnp.dot(mixed, out_weight, preferred_element_type=F32).astype(BF16), residual_in, norm_gain
    )
    count, lanes = lax.axis_size("seq"), lax.axis_size("tp")
    group = count // EXPERTS
    capacity = 3 * rows // EXPERTS
    spread = lanes * capacity
    target, prob = routing(both)
    placing = jnp.sum(
        (jnp.arange(EXPERTS * spread, dtype=jnp.int32)[:, None, None] == target[None]).astype(BF16),
        axis=2,
    )
    column = jnp.arange(count * spread, dtype=jnp.int32)
    column = column // (spread * group) * spread + column % spread
    pick = (target.T.reshape(-1)[:, None] == column[None, :]).astype(BF16)
    arrived = dispatch(placing, normed_part.reshape(tokens, width // lanes), group)
    share = expert_share(arrived, up_weight, down_weight)
    return (mixer_out, bring_back(share, pick, prob.T.reshape(-1, 1), mixer_out))


def solution(mesh):
    return jax.shard_map(
        per_device,
        mesh=mesh,
        in_specs=(
            P("seq", "tp"),
            P("seq", "tp"),
            P(None, "tp"),
            P("tp"),
            P("tp", None),
            P(None, "tp"),
            P("tp"),
            P("tp", None),
            P("tp"),
            P("tp", None),
            P(("seq", "tp"), None),
            P(),
            P(("seq", "tp"), None),
            P(("seq", "tp"), None),
            P(None, ("seq", "tp")),
            P(("seq", "tp"), None),
        ),
        out_specs=(P(("seq", "tp"), None), P(("seq", "tp"), None)),
        check_vma=False,
    )
```

```python
import functools

import jax
import jax.numpy as jnp
from jax import lax
from jax.experimental import pallas as pl
from jax.experimental.pallas import tpu as pltpu
from jax.sharding import PartitionSpec as P

STATE = 16
DTRANK = 512
EXPERTS = 8
MESH = pl.DeviceIdType.MESH
VMEM_SPEC = pl.BlockSpec(memory_space=pltpu.VMEM)
SMEM_SPEC = pl.BlockSpec(memory_space=pltpu.SMEM)
F32 = jnp.float32
BF16 = jnp.bfloat16
MIB = 1024 * 1024
AHEAD = 3
LAG = 2


def shifted(value, axis, steps):
    count = lax.axis_size(axis)
    initial, last = (max(0, -steps), min(count, count - steps))
    return lax.ppermute(value, axis, [(source, source + steps) for source in range(initial, last)])


def greet(peers):
    barrier = pltpu.get_barrier_semaphore()
    for peer in peers:
        pl.semaphore_signal(barrier, inc=1, device_id=peer, device_id_type=MESH)
    pl.semaphore_wait(barrier, len(peers))


def send(source, target, send_sem, recv_sem, device):
    return pltpu.make_async_remote_copy(
        src_ref=source,
        dst_ref=target,
        send_sem=send_sem,
        recv_sem=recv_sem,
        device_id=device,
        device_id_type=MESH,
    )


def bit_of(index, stage):
    return lax.rem(index // 2**stage, 2)


def flipped(index, stage):
    return index + 2**stage - 2 * 2**stage * bit_of(index, stage)


def stages_of(count):
    return count.bit_length() - 1


def sum_kernel(
    count,
    part_ref,
    route_ref,
    out_ref,
    routes_ref,
    outgoing,
    arriving,
    send_sems,
    recv_sems,
    route_send_sems,
    route_recv_sems,
):
    me = lax.axis_index("tp")
    stages = stages_of(count)
    greet([{"tp": lax.rem(me + d, count)} for d in range(1, count)])
    routes = [
        send(
            route_ref,
            routes_ref.at[me],
            route_send_sems.at[d],
            route_recv_sems.at[d],
            {"tp": lax.rem(me + d, count)},
        )
        for d in range(1, count)
    ]
    for k in range(stages):
        source = part_ref if k == 0 else outgoing
        copy = send(
            source, arriving.at[k], send_sems.at[k], recv_sems.at[k], {"tp": flipped(me, k)}
        )
        copy.start()
        if k == 0:
            for route in routes:
                route.start()
            routes_ref[me] = route_ref[...]
        copy.wait()
        total = source[...].astype(F32) + arriving[k].astype(F32)
        if k < stages - 1:
            outgoing[...] = total.astype(BF16)
        else:
            out_ref[...] = total
    for route in routes:
        route.wait()


def sum_over_tp(part, route):
    count = lax.axis_size("tp")
    stages = stages_of(count)
    return pl.pallas_call(
        functools.partial(sum_kernel, count),
        out_shape=(
            jax.ShapeDtypeStruct(part.shape, F32),
            jax.ShapeDtypeStruct((count, *route.shape), F32),
        ),
        in_specs=[VMEM_SPEC] * 2,
        out_specs=(VMEM_SPEC, VMEM_SPEC),
        scratch_shapes=[
            pltpu.VMEM(part.shape, BF16),
            pltpu.VMEM((stages, *part.shape), BF16),
            pltpu.SemaphoreType.DMA((stages,)),
            pltpu.SemaphoreType.DMA((stages,)),
            pltpu.SemaphoreType.DMA((count,)),
            pltpu.SemaphoreType.DMA((count,)),
        ],
        compiler_params=pltpu.CompilerParams(collective_id=0, has_side_effects=True),
        name="projection_sum",
    )(part, route)


def scan_kernel(
    count,
    step_ref,
    inner_ref,
    maps_ref,
    rate_ref,
    out_ref,
    state,
    outgoing,
    arriving,
    send_sems,
    recv_sems,
):
    me = lax.axis_index("seq")
    tokens = step_ref.shape[0]
    tile = step_ref.shape[1:]
    greet([{"seq": lax.rem(me + d, count)} for d in range(1, count)])

    def advance(t, states):
        step = step_ref[t]
        drive = step * inner_ref[t]
        return step, tuple(
            jnp.exp(step * rate_ref[n]) * states[n] + maps_ref[t, n] * drive for n in range(STATE)
        )

    def ending(t, carried):
        states, total = carried
        step, states = advance(t, states)
        return states, total + step

    zero = jnp.zeros(tile, F32)
    states, total = lax.fori_loop(0, tokens, ending, ((zero,) * STATE, zero), unroll=4)
    for n in range(STATE):
        outgoing[n] = states[n].astype(BF16)
    upper = total.astype(BF16)
    outgoing[STATE] = upper
    outgoing[STATE + 1] = (total - upper.astype(F32)).astype(BF16)

    def copy_by(d):
        return send(
            outgoing,
            arriving.at[d],
            send_sems.at[d],
            recv_sems.at[d],
            {"seq": lax.rem(me + d, count)},
        )

    for d in range(1, count):

        @pl.when(me + d < count)
        def _():
            copy_by(d).start()

    state[...] = jnp.zeros(state.shape, F32)
    for d in range(count - 1, 0, -1):

        @pl.when(me >= d)
        def _():
            copy_by(d).wait_recv()
            passed = arriving[d, STATE].astype(F32) + arriving[d, STATE + 1].astype(F32)
            for n in range(STATE):
                state[n] = jnp.exp(passed * rate_ref[n]) * state[n] + arriving[d, n].astype(F32)

    def reading(t, states):
        _, states = advance(t, states)
        terms = [maps_ref[t, STATE + n] * states[n] for n in range(STATE)]
        while len(terms) > 1:
            terms = [a + b for a, b in zip(terms[::2], terms[1::2])]
        out_ref[t] = terms[0]
        return states

    lax.fori_loop(0, tokens, reading, tuple(state[n] for n in range(STATE)), unroll=4)
    for d in range(1, count):

        @pl.when(me + d < count)
        def _():
            copy_by(d).wait_send()


def recur(step_size, inner, maps, decay_rate):
    count = lax.axis_size("seq")
    tokens, channels = step_size.shape
    tile = (channels // 128, 128)
    rate = -decay_rate.T.reshape(STATE, *tile)
    out = pl.pallas_call(
        functools.partial(scan_kernel, count),
        out_shape=jax.ShapeDtypeStruct((tokens, *tile), F32),
        in_specs=[VMEM_SPEC, VMEM_SPEC, SMEM_SPEC, VMEM_SPEC],
        out_specs=VMEM_SPEC,
        scratch_shapes=[
            pltpu.VMEM((STATE, *tile), F32),
            pltpu.VMEM((STATE + 2, *tile), BF16),
            pltpu.VMEM((count, STATE + 2, *tile), BF16),
            pltpu.SemaphoreType.DMA((count,)),
            pltpu.SemaphoreType.DMA((count,)),
        ],
        compiler_params=pltpu.CompilerParams(
            collective_id=1, has_side_effects=True, vmem_limit_bytes=24 * MIB
        ),
        name="recurrence",
    )(step_size.reshape(tokens, *tile), inner.reshape(tokens, *tile), maps, rate)
    return out.reshape(tokens, channels)


def mixer_kernel(count, part_ref, residual_ref, gain_ref, mixer_ref, normed_ref, *scratch):
    stages = stages_of(count)
    works, arrivings = scratch[:stages], scratch[stages : 2 * stages]
    columns, send_sems, recv_sems, gather_send_sems, gather_recv_sems = scratch[2 * stages :]
    me = lax.axis_index("tp")
    greet([{"tp": lax.rem(me + d, count)} for d in range(1, count)])
    total = None
    for k in range(stages):
        source = part_ref if k == 0 else works[k]
        kept = count // 2 ** (k + 1)
        bit = bit_of(me, k)
        copies = [
            send(
                source.at[2 * i + 1 - bit],
                arrivings[k].at[i],
                send_sems.at[k, i],
                recv_sems.at[k, i],
                {"tp": flipped(me, k)},
            )
            for i in range(kept)
        ]
        for copy in copies:
            copy.start()
        for i, copy in enumerate(copies):
            copy.wait()
            total = source[2 * i + bit].astype(F32) + arrivings[k][i].astype(F32)
            if k < stages - 1:
                works[k + 1][i] = total.astype(BF16)
    mixer = (total + residual_ref[...].astype(F32)).astype(BF16)
    mixer_ref[...] = mixer
    wide = mixer.astype(F32)
    normed = (
        wide * lax.rsqrt(jnp.mean(wide * wide, axis=1, keepdims=True) + 1e-06) * gain_ref[...]
    ).astype(BF16)
    part_width = columns.shape[2]
    for j in range(count):
        columns[j] = normed[:, j * part_width : (j + 1) * part_width]
    copies = []
    for d in range(1, count):
        peer = lax.rem(me + d, count)
        copies.append(
            send(
                columns.at[peer],
                normed_ref.at[me],
                gather_send_sems.at[d],
                gather_recv_sems.at[d],
                {"tp": peer},
            )
        )
    for copy in copies:
        copy.start()
    normed_ref[me] = columns[me]
    for copy in copies:
        copy.wait()


def mixer_rows(part, residual, gain):
    count = lax.axis_size("tp")
    stages = stages_of(count)
    rows, width = residual.shape
    sems = pltpu.SemaphoreType.DMA((stages, count // 2))
    return pl.pallas_call(
        functools.partial(mixer_kernel, count),
        out_shape=(
            jax.ShapeDtypeStruct((rows, width), BF16),
            jax.ShapeDtypeStruct((count, rows, width // count), BF16),
        ),
        in_specs=[VMEM_SPEC] * 3,
        out_specs=(VMEM_SPEC, VMEM_SPEC),
        scratch_shapes=[pltpu.VMEM((count // 2**k, rows, width), BF16) for k in range(stages)]
        + [pltpu.VMEM((count // 2 ** (k + 1), rows, width), BF16) for k in range(stages)]
        + [pltpu.VMEM((count, rows, width // count), BF16)]
        + [sems] * 2
        + [pltpu.SemaphoreType.DMA((count,))] * 2,
        compiler_params=pltpu.CompilerParams(
            collective_id=2, has_side_effects=True, vmem_limit_bytes=32 * MIB
        ),
        name="mixer_sum",
    )(part.reshape(count, rows, width), residual, gain.reshape(1, width))


def dispatch_kernel(
    count,
    lanes,
    group,
    placing_ref,
    normed_ref,
    out_ref,
    slots,
    send_sems,
    recv_sems,
    spread_send_sems,
    spread_recv_sems,
):
    me, lane = lax.axis_index("seq"), lax.axis_index("tp")
    stages = stages_of(lanes)
    capacity, part_width = slots.shape[1:]
    greet(
        [{"seq": lax.rem(me + d, count)} for d in range(1, count)]
        + [{"tp": flipped(lane, k)} for k in range(stages)]
    )

    def block(source, column):
        return (
            pl.ds(pl.multiple_of(source * capacity, 16), capacity),
            pl.ds(pl.multiple_of(column * part_width, 128), part_width),
        )

    placed = jnp.dot(placing_ref[...], normed_ref[...], preferred_element_type=F32).astype(BF16)
    for e in range(EXPERTS):
        slots[e] = placed[e * capacity : (e + 1) * capacity]
    firsts = []
    for d in range(1, count):
        target = lax.rem(me + d, count)
        firsts.append(
            send(
                slots.at[target // group],
                out_ref.at[block(me, lane)],
                send_sems.at[d],
                recv_sems.at[d],
                {"seq": target},
            )
        )
        if d <= AHEAD:
            firsts[-1].start()
    out_ref[block(me, lane)] = slots[me // group]

    spread = {}
    for step in range(count + LAG * (stages - 1)):
        for k in range(stages - 1, -1, -1):
            d = step - LAG * (stages - 1 - k)
            if d < 0 or d >= count:
                continue
            if k == stages - 1:
                if d > 0:
                    firsts[d - 1].wait_recv()
                    if d + AHEAD < count:
                        firsts[d - 1 + AHEAD].start()
            else:
                for copy in spread[d, k + 1]:
                    copy.wait_recv()
            source = lax.rem(me - d + count, count)
            low = lax.rem(lane, 2 ** (k + 1))
            spread[d, k] = []
            for i in range(lanes // 2 ** (k + 1)):
                place = out_ref.at[block(source, low + 2 ** (k + 1) * i)]
                copy = send(
                    place,
                    place,
                    spread_send_sems.at[d, k, i],
                    spread_recv_sems.at[d, k, i],
                    {"tp": flipped(lane, k)},
                )
                copy.start()
                spread[d, k].append(copy)
    for copy in firsts:
        copy.wait_send()
    for (_, k), copies in spread.items():
        for copy in copies:
            copy.wait_send()
            if k == 0:
                copy.wait_recv()


def dispatch(placing, normed, group):
    count, lanes = lax.axis_size("seq"), lax.axis_size("tp")
    stages = stages_of(lanes)
    capacity = placing.shape[0] // EXPERTS
    part_width = normed.shape[1]
    return pl.pallas_call(
        functools.partial(dispatch_kernel, count, lanes, group),
        out_shape=jax.ShapeDtypeStruct((count * capacity, lanes * part_width), BF16),
        in_specs=[VMEM_SPEC] * 2,
        out_specs=VMEM_SPEC,
        scratch_shapes=[pltpu.VMEM((EXPERTS, capacity, part_width), BF16)]
        + [pltpu.SemaphoreType.DMA((count,))] * 2
        + [pltpu.SemaphoreType.DMA((count, stages, lanes // 2))] * 2,
        compiler_params=pltpu.CompilerParams(
            collective_id=3, has_side_effects=True, vmem_limit_bytes=32 * MIB
        ),
        name="dispatch",
    )(placing, normed)


def return_kernel(
    count, lanes, part_ref, pick_ref, prob_ref, mixer_ref, out_ref, *scratch
):
    stages = stages_of(lanes)
    works, arrivings = scratch[:stages], scratch[stages : 2 * stages]
    home, outgoing, incoming = scratch[2 * stages : 2 * stages + 3]
    sum_send, sum_recv, home_send, home_recv, row_send, row_recv = scratch[2 * stages + 3 :]
    me, lane = lax.axis_index("seq"), lax.axis_index("tp")
    capacity, part_width = home.shape[1:]
    greet(
        [{"seq": lax.rem(me + d, count)} for d in range(1, count)]
        + [{"tp": lax.rem(lane + d, lanes)} for d in range(1, lanes)]
    )

    def block(d, column):
        target = lax.rem(me + d, count)
        return (
            pl.ds(pl.multiple_of(target * capacity, 16), capacity),
            pl.ds(pl.multiple_of(column * part_width, 128), part_width),
        )

    def start(d, k):
        bit = bit_of(lane, k)
        copies = []
        for i in range(lanes // 2 ** (k + 1)):
            index = 2 * i + 1 - bit
            source = part_ref.at[block(d, index)] if k == 0 else works[k - 1].at[d, index]
            copy = send(
                source,
                arrivings[k].at[d, i],
                sum_send.at[d, k, i],
                sum_recv.at[d, k, i],
                {"tp": flipped(lane, k)},
            )
            copy.start()
            copies.append(copy)
        return copies

    def finish(d, k, copies):
        bit = bit_of(lane, k)
        for i, copy in enumerate(copies):
            copy.wait_recv()
            index = 2 * i + bit
            mine = part_ref[block(d, index)] if k == 0 else works[k - 1][d, index]
            works[k][d, i] = (mine.astype(F32) + arrivings[k][d, i].astype(F32)).astype(BF16)

    order = list(range(1, count)) + [0]
    sums = {(d, 0): start(d, 0) for d in order}
    homes = []
    for step in range(count + LAG * (stages - 1)):
        for k in range(stages):
            if step - LAG * k < 0 or step - LAG * k >= count:
                continue
            d = order[step - LAG * k]
            finish(d, k, sums[d, k])
            if k < stages - 1:
                sums[d, k + 1] = start(d, k + 1)
            elif d == 0:
                home[me] = works[k][0, 0]
            else:
                copy = send(
                    works[k].at[d, 0],
                    home.at[me],
                    home_send.at[d],
                    home_recv.at[d],
                    {"seq": lax.rem(me + d, count)},
                )
                copy.start()
                homes.append(copy)
    for copy in homes:
        copy.wait_recv()
    arrived = home[...].reshape(count * capacity, part_width)
    picked = jnp.dot(pick_ref[...], arrived, preferred_element_type=F32) * prob_ref[...]
    half = picked.shape[0] // 2
    outgoing[...] = (picked[:half] + picked[half:]).astype(BF16).reshape(outgoing.shape)
    rows = []
    for d in range(1, lanes):
        peer = lax.rem(lane + d, lanes)
        copy = send(
            outgoing.at[peer], incoming.at[lane], row_send.at[d], row_recv.at[d], {"tp": peer}
        )
        copy.start()
        rows.append(copy)
    incoming[lane] = outgoing[lane]
    for copy in rows:
        copy.wait()
    for j in range(lanes):
        span = slice(j * part_width, (j + 1) * part_width)
        out_ref[:, span] = (mixer_ref[:, span].astype(F32) + incoming[j].astype(F32)).astype(BF16)
    for copy in homes:
        copy.wait_send()
    for copies in sums.values():
        for copy in copies:
            copy.wait_send()


def bring_back(part, pick, prob, mixer):
    count, lanes = lax.axis_size("seq"), lax.axis_size("tp")
    stages = stages_of(lanes)
    rows, width = mixer.shape
    block = (part.shape[0] // count, width // lanes)
    sums = [
        pltpu.VMEM((count, lanes // 2 ** (k + 1), *block), BF16) for _ in range(2) for k in range(stages)
    ]
    return pl.pallas_call(
        functools.partial(return_kernel, count, lanes),
        out_shape=jax.ShapeDtypeStruct((rows, width), BF16),
        in_specs=[VMEM_SPEC] * 4,
        out_specs=VMEM_SPEC,
        scratch_shapes=sums
        + [pltpu.VMEM((count, *block), BF16)]
        + [pltpu.VMEM((lanes, rows, block[1]), BF16)] * 2
        + [pltpu.SemaphoreType.DMA((count, stages, lanes // 2))] * 2
        + [pltpu.SemaphoreType.DMA((count,))] * 2
        + [pltpu.SemaphoreType.DMA((lanes,))] * 2,
        compiler_params=pltpu.CompilerParams(
            collective_id=4, has_side_effects=True, vmem_limit_bytes=40 * MIB
        ),
        name="bring_back",
    )(part, pick, prob, mixer)


def expert_share(arrived_flat, up_weight, down_weight):
    hidden = jax.nn.silu(jnp.dot(arrived_flat, up_weight, preferred_element_type=F32)).astype(BF16)
    return jnp.dot(hidden, down_weight, preferred_element_type=F32).astype(BF16)


def routing(both):
    lanes, rows = both.shape[:2]
    capacity = 3 * rows // EXPERTS
    chosen = both[:, :, :2].astype(jnp.int32).reshape(lanes, rows * 2)
    hits = (chosen[:, :, None] == jnp.arange(EXPERTS, dtype=jnp.int32)).astype(jnp.int32)
    earlier = jnp.cumsum(hits, axis=1) - hits
    slot = jnp.sum(earlier * hits, axis=2)
    source = jnp.arange(lanes, dtype=jnp.int32)[:, None]
    target = (chosen * lanes + source) * capacity + slot
    return target.reshape(lanes * rows, 2), both[:, :, 2:].reshape(lanes * rows, 2)


def per_device(
    x_in,
    gate_in,
    conv_weight,
    conv_bias,
    x_weight,
    dt_weight,
    dt_bias,
    decay_rate,
    skip_gain,
    out_weight,
    residual_in,
    norm_gain,
    expert_ids,
    gate_prob,
    up_weight,
    down_weight,
):
    tokens, channels = x_in.shape
    width = out_weight.shape[1]
    reach = conv_weight.shape[0] - 1
    rim_rows = shifted(x_in[tokens - reach :], "seq", 1)
    padded = jnp.concatenate([rim_rows, x_in], axis=0).astype(F32)
    conv_out = conv_bias[None, :] + sum(
        (
            conv_weight[offset][None, :] * padded[offset : offset + tokens]
            for offset in range(reach + 1)
        )
    )
    inner = jax.nn.silu(conv_out).astype(BF16)
    projected, both = sum_over_tp(
        jnp.dot(inner, x_weight, preferred_element_type=F32).astype(BF16),
        jnp.concatenate([expert_ids.astype(F32), gate_prob], axis=1),
    )
    dt_low = projected[:, :DTRANK].astype(BF16)
    step_size = jax.nn.softplus(
        jnp.dot(dt_low, dt_weight, preferred_element_type=F32) + dt_bias[None, :]
    )
    ssm = recur(step_size, inner.astype(F32), projected[:, DTRANK:], decay_rate)
    mixed = (
        (ssm + skip_gain[None, :] * inner.astype(F32)) * jax.nn.silu(gate_in.astype(F32))
    ).astype(BF16)
    rows = tokens // lax.axis_size("tp")
    mixer_out, normed_part = mixer_rows(
        jnp.dot(mixed, out_weight, preferred_element_type=F32).astype(BF16), residual_in, norm_gain
    )
    count, lanes = lax.axis_size("seq"), lax.axis_size("tp")
    group = count // EXPERTS
    capacity = 3 * rows // EXPERTS
    spread = lanes * capacity
    target, prob = routing(both)
    placing = jnp.sum(
        (jnp.arange(EXPERTS * spread, dtype=jnp.int32)[:, None, None] == target[None]).astype(BF16),
        axis=2,
    )
    column = jnp.arange(count * spread, dtype=jnp.int32)
    column = column // (spread * group) * spread + column % spread
    pick = (target.T.reshape(-1)[:, None] == column[None, :]).astype(BF16)
    arrived = dispatch(placing, normed_part.reshape(tokens, width // lanes), group)
    share = expert_share(arrived, up_weight, down_weight)
    return (mixer_out, bring_back(share, pick, prob.T.reshape(-1, 1), mixer_out))


def solution(mesh):
    return jax.shard_map(
        per_device,
        mesh=mesh,
        in_specs=(
            P("seq", "tp"),
            P("seq", "tp"),
            P(None, "tp"),
            P("tp"),
            P("tp", None),
            P(None, "tp"),
            P("tp"),
            P("tp", None),
            P("tp"),
            P("tp", None),
            P(("seq", "tp"), None),
            P(),
            P(("seq", "tp"), None),
            P(("seq", "tp"), None),
            P(None, ("seq", "tp")),
            P(("seq", "tp"), None),
        ),
        out_specs=(P(("seq", "tp"), None), P(("seq", "tp"), None)),
        check_vma=False,
    )
```
